512 devices in a mesh: layer: 8 (over z_hi, core), feat: 64 (over x, y, z_lo).
Axes of the slice: x: 4, y: 8, z: 8 (z_hi: 4, z_lo: 2; z = z_hi * 2 + z_lo), core: 2. Of those that a mesh axis runs over, the one named last changes fastest.
Arguments:
- source: float32 [8, 256, 2048], P('layer', 'feat'), may hold values from -6 to 6
- w_enc: bfloat16 [8, 2048, 24576], P('layer', None, 'feat'), may hold values from -0.125 to 0.125
- b_enc: float32 [8, 24576], P('layer', 'feat'), may hold values from -3 to 3
- threshold: float32 [8, 24576], P('layer', 'feat'), may hold values from 0.2 to 2
- dec_self: bfloat16 [8, 24576, 2048], P('layer', 'feat'), may hold values from -0.0390625 to 0.0390625
- dec_next: bfloat16 [8, 24576, 2048], P('layer', 'feat'), may hold values from -0.0390625 to 0.0390625
- target: float32 [8, 256, 2048], P('layer', 'feat'), may hold values from -3 to 3
Outputs:
- residual: float32 [8, 256, 2048], P('layer', 'feat')
The draws below stay inside these ranges and needn't reach their ends.
All inputs are finite; a program needn't handle non-finite values.
Results may differ from the reference program's by a relative error of at most 0.0038.
Values may be sent and summed in bfloat16 or wider, within the bound.
A program may use at most 64 MiB of HBM per device.

```python
import math
import jax
import jax.numpy as jnp
from jax import lax

D = 2048
F = 24576
ROWS = 256
LAYERS = 8


def block_scale(rng, dims, pieces, low, largest):
    loudness, own = 1.0, jax.random.fold_in(rng, 6)
    for axis_at, parts in pieces:
        steps = jnp.exp(jax.random.uniform(jax.random.fold_in(own, axis_at), (parts,), jnp.float32, low / len(pieces), largest / len(pieces)))
        loudness = loudness * jnp.repeat(steps, dims[axis_at] // parts).reshape([-1 if axis == axis_at else 1 for axis in range(len(dims))])
    return loudness


def scatter_about(key, extent, width, reach, cuts=(), dtype=jnp.bfloat16):
    drawn = width * jax.random.normal(key, extent, jnp.float32)
    if cuts:
        drawn = drawn * block_scale(key, extent, cuts, -0.22, 0.18)
    return jnp.clip(drawn, -reach, reach).astype(dtype)


def setup_inputs(seed: int = 0) -> dict:
    key_of = jax.random.split(jax.random.key(seed), 8)
    source = scatter_about(key_of[0], (LAYERS, ROWS, D), 1.0, 6.0, ((0, 8), (1, 64)), jnp.float32)
    w_enc = scatter_about(key_of[1], (LAYERS, D, F), D ** -0.5, 0.125, ((0, 8), (2, 64)))
    b_enc = scatter_about(key_of[2], (LAYERS, F), 0.5, 3.0, ((0, 8), (1, 64)), jnp.float32)
    threshold = jnp.clip(jnp.exp(math.log(2.0) - 2.3025851 * jax.random.uniform(key_of[3], (LAYERS, F), jnp.float32) ** block_scale(key_of[3], (LAYERS, F), ((0, 8), (1, 64)), -0.2, 0.2)), 0.2, 2.0)
    dec_self = scatter_about(key_of[4], (LAYERS, F, D), F ** -0.5, 0.0390625, ((0, 8), (1, 64)))
    dec_next = scatter_about(key_of[5], (LAYERS, F, D), F ** -0.5, 0.0390625, ((0, 8), (1, 64)))
    target = scatter_about(key_of[6], (LAYERS, ROWS, D), 0.5, 3.0, ((0, 8), (1, 64)), jnp.float32)
    return dict(source=source, w_enc=w_enc, b_enc=b_enc, threshold=threshold, dec_self=dec_self, dec_next=dec_next, target=target)


def section(inputs):
    rows, enc, bias, thr, dec_own, dec_after = inputs
    scale = lax.rsqrt(lax.optimization_barrier(jnp.mean(rows * rows, axis=1, keepdims=True)) + 1e-05)
    normed = (rows * scale).astype(jnp.bfloat16)
    pre = jnp.dot(normed, enc, preferred_element_type=jnp.float32) + bias
    codes = (pre * jax.nn.sigmoid((pre - thr) / 0.1)).astype(jnp.bfloat16)
    own = jnp.dot(codes, dec_own, preferred_element_type=jnp.float32)
    carried = jnp.dot(codes, dec_after, preferred_element_type=jnp.float32)
    return (own, carried)

def reference(source, w_enc, b_enc, threshold, dec_self, dec_next, target):
    own, carried = lax.map(section, (source, w_enc, b_enc, threshold, dec_self, dec_next))
    shifted = jnp.concatenate([jnp.zeros_like(carried[:1]), carried[:-1]], axis=0)
    return own + shifted - target
```

```python
import jax
import jax.numpy as jnp
from jax import lax
from jax.experimental import pallas as pl
from jax.experimental.pallas import tpu as pltpu
from jax.sharding import PartitionSpec as P

MESH = pl.DeviceIdType.MESH
D = 2048
HALF = 1024
FEATS = 384
W3 = 3 * HALF
MID = W3 // 2
PIECES = (
    (0, 0), (0, 1), (1, 0), (-1, 0), (1, 1), (-1, 1), (2, 0), (-2, 0),
    (2, 1), (-2, 1), (3, 0), (-3, 0), (3, 1), (-3, 1), (4, 0), (4, 1),
)
NQ = 16
NH = 2
PER = NQ // NH
XR = PER * 4
HR = 4 * XR
RELAY = (True, False)


def kernel(
    source, w_enc, b_enc, threshold, dec_self, dec_next, target, out,
    rows, wv, bv, tv, tgt, dbuf, piece, xa, cod, cod_o, acc,
    xs, xin, relay, zs, zr, own, fin, fin_in,
    lsem, ag_s, ag_r, ax_s, ax_r, dw_s, dw_r, cx_s, cx_r, rx_s, rx_r, rz_s, rz_r, f_s, f_r,
):
    layer, feat = lax.axis_index("layer"), lax.axis_index("feat")
    zh, c = layer // 2, layer % 2
    x, y, z = feat // 16, (feat // 2) % 8, feat % 2

    def at(dx=0, dy=0, dz=0, core=None, dzh=0):
        core = c if core is None else core
        where = lax.rem(zh + dzh + 4, 4) * 2 + core
        place = lax.rem(x + dx + 4, 4) * 16 + lax.rem(y + dy + 8, 8) * 2
        return (where, place + (1 - z if dz else z))

    partner = at(core=1 - c)

    def remote(src, dst, send, recv, to):
        return pltpu.make_async_remote_copy(
            src_ref=src, dst_ref=dst, send_sem=send, recv_sem=recv, device_id=to, device_id_type=MESH
        )

    mine = pl.ds(pl.multiple_of(c * HALF, HALF), HALF)
    theirs = pl.ds(pl.multiple_of((1 - c) * HALF, HALF), HALF)
    loads = [
        pltpu.make_async_copy(source.at[0], rows, lsem.at[0]),
        pltpu.make_async_copy(w_enc.at[0], wv, lsem.at[1]),
        pltpu.make_async_copy(b_enc, bv, lsem.at[2]),
        pltpu.make_async_copy(threshold, tv, lsem.at[3]),
        pltpu.make_async_copy(dec_self.at[0, :, mine], dbuf.at[c], lsem.at[4]),
        pltpu.make_async_copy(dec_next.at[0, :, mine], dbuf.at[1 - c], lsem.at[5]),
        pltpu.make_async_copy(target.at[0], tgt, lsem.at[6]),
    ]
    for load in loads:
        load.start()

    barrier = pltpu.get_barrier_semaphore()
    peers = [at(dy=dy, dz=dz) for dy, dz in PIECES[1:]] + [at(dx=d) for d in (1, 2, 3)]
    peers += [partner, at(core=0, dzh=-1), at(core=1, dzh=-1)]
    for peer in peers:
        pl.semaphore_signal(barrier, inc=1, device_id=peer, device_id_type=MESH)

    loads[0].wait()
    r = rows[...]
    scale = lax.rsqrt(jnp.mean(r * r, axis=1, keepdims=True) + 1e-05)
    piece[0] = (r * scale).astype(jnp.bfloat16)
    pl.semaphore_wait(barrier, len(peers))

    sent = []

    def go(copy):
        copy.start()
        sent.append(copy)
        return copy

    gather = [None] + [
        remote(piece.at[0], piece.at[q], ag_s.at[q], ag_r.at[q], at(dy=PIECES[q][0], dz=PIECES[q][1]))
        for q in range(1, NQ)
    ]
    for q in reversed(range(1, NQ)):
        go(gather[q])
    lent = [
        remote(dec_self.at[0, :, theirs], dbuf.at[3 - c], dw_s.at[0], dw_r.at[0], partner),
        remote(dec_next.at[0, :, theirs], dbuf.at[2 + c], dw_s.at[1], dw_r.at[1], partner),
    ]
    for copy in lent:
        go(copy)

    spread = []
    for h in range(NH):
        for q in range(h * PER, (h + 1) * PER):
            if q:
                gather[q].wait_recv()
        block = jnp.concatenate([piece[q] for q in range(h * PER, (h + 1) * PER)], axis=0)
        xa[h, 0:XR, :] = block
        mineblock = xa.at[h, 0:XR]
        nxt = remote(mineblock, xa.at[h, 3 * XR:4 * XR], ax_s.at[h, 0], ax_r.at[h, 0], at(dx=1))
        prv = remote(mineblock, xa.at[h, XR:2 * XR], ax_s.at[h, 1], ax_r.at[h, 1], at(dx=-1))
        if RELAY[h]:
            a = remote(
                xa.at[h, 3 * XR:4 * XR, 0:HALF], xa.at[h, 2 * XR:3 * XR, 0:HALF],
                ax_s.at[h, 2], ax_r.at[h, 2], at(dx=1),
            )
            b = remote(
                xa.at[h, XR:2 * XR, HALF:D], xa.at[h, 2 * XR:3 * XR, HALF:D],
                ax_s.at[h, 3], ax_r.at[h, 3], at(dx=-1),
            )
            go(nxt)
            go(prv)
            spread.append((nxt, prv, a, b))
        else:
            opp = remote(mineblock, xa.at[h, 2 * XR:3 * XR], ax_s.at[h, 2], ax_r.at[h, 2], at(dx=2))
            go(opp)
            go(nxt)
            go(prv)
            spread.append((nxt, prv, opp))

    def relays(h):
        if RELAY[h]:
            nxt, prv, a, b = spread[h]
            nxt.wait_recv()
            go(a)
            prv.wait_recv()
            go(b)

    def arrived(h):
        if RELAY[h]:
            spread[h][2].wait_recv()
            spread[h][3].wait_recv()
        else:
            for copy in spread[h]:
                copy.wait_recv()

    def encode(h):
        pre = jnp.dot(xa[h], wv[...], preferred_element_type=jnp.float32) + bv[...]
        cod[h] = (pre * jax.nn.sigmoid((pre - tv[...]) / 0.1)).astype(jnp.bfloat16)
        copy = remote(cod.at[h], cod_o.at[h], cx_s.at[h], cx_r.at[h], partner)
        return go(copy)

    def scatter_x(h):
        def part(d, lo, hi):
            return acc[h, d * XR:(d + 1) * XR, lo:hi]

        xs[h, 0] = part(2, 0, MID).astype(jnp.bfloat16)
        xs[h, 1] = part(2, MID, W3).astype(jnp.bfloat16)
        far = [
            go(remote(xs.at[h, 0], xin.at[h, 0], rx_s.at[h, 0], rx_r.at[h, 0], at(dx=1))),
            go(remote(xs.at[h, 1], xin.at[h, 1], rx_s.at[h, 1], rx_r.at[h, 1], at(dx=-1))),
        ]
        xs[h, 2] = part(1, MID, W3).astype(jnp.bfloat16)
        xs[h, 3] = part(3, 0, MID).astype(jnp.bfloat16)
        near = [
            go(remote(xs.at[h, 2], xin.at[h, 2], rx_s.at[h, 2], rx_r.at[h, 2], at(dx=1))),
            go(remote(xs.at[h, 3], xin.at[h, 3], rx_s.at[h, 3], rx_r.at[h, 3], at(dx=-1))),
        ]
        return far, near

    def relay_x(h, far):
        out_ = []
        for i, (d, lo, hi) in enumerate(((1, 0, MID), (3, MID, W3))):
            far[i].wait_recv()
            relay[h, i] = (acc[h, d * XR:(d + 1) * XR, lo:hi] + xin[h, i].astype(jnp.float32)).astype(jnp.bfloat16)
            out_.append(
                go(remote(relay.at[h, i], xin.at[h, 4 + i], rx_s.at[h, 4 + i], rx_r.at[h, 4 + i], at(dx=1 if i == 0 else -1)))
            )
        return out_

    def scatter_zy(h, near, last):
        for copy in near + last:
            copy.wait_recv()
        f = jnp.float32
        left = acc[h, 0:XR, 0:MID] + (xin[h, 4].astype(f) + xin[h, 3].astype(f))
        right = acc[h, 0:XR, MID:W3] + (xin[h, 2].astype(f) + xin[h, 5].astype(f))
        for i in range(PER):
            q = h * PER + i
            if q == 0:
                own[:, 0:MID] = left[0:4]
                own[:, MID:W3] = right[0:4]
                continue
            zs[q, :, 0:MID] = left[4 * i:4 * i + 4].astype(jnp.bfloat16)
            zs[q, :, MID:W3] = right[4 * i:4 * i + 4].astype(jnp.bfloat16)
        copies = []
        for i in reversed(range(PER)):
            q = h * PER + i
            if q:
                dy, dz = PIECES[q]
                copies.append((q, go(remote(zs.at[q], zr.at[q], rz_s.at[q], rz_r.at[q], at(dy=-dy, dz=dz)))))
        return copies

    relays(0)
    for i in (1, 2, 3):
        loads[i].wait()
    arrived(0)
    codes = [encode(0)]
    loads[4].wait()
    loads[5].wait()
    acc[0, :, 0:HALF] = jnp.dot(cod[0], dbuf[0], preferred_element_type=jnp.float32)
    for copy in lent:
        copy.wait_recv()

    def decode(h, first):
        if first:
            acc[h, :, 0:HALF] = jnp.dot(cod[h], dbuf[0], preferred_element_type=jnp.float32)
        near_part = jnp.dot(cod[h], dbuf[1], preferred_element_type=jnp.float32)
        codes[h].wait_recv()
        acc[h, :, HALF:2 * HALF] = near_part + jnp.dot(cod_o[h], dbuf[2], preferred_element_type=jnp.float32)
        acc[h, :, 2 * HALF:W3] = jnp.dot(cod_o[h], dbuf[3], preferred_element_type=jnp.float32)

    decode(0, False)
    far0, near0 = scatter_x(0)
    relays(1)
    arrived(1)
    codes.append(encode(1))
    last0 = relay_x(0, far0)
    decode(1, True)
    far1, near1 = scatter_x(1)
    z0 = scatter_zy(0, near0, last0)
    last1 = relay_x(1, far1)
    z1 = scatter_zy(1, near1, last1)

    total = own[...]
    for q, copy in z0 + z1:
        copy.wait_recv()
        total = total + zr[q].astype(jnp.float32)
    fin[0] = total[:, 0:HALF]
    fin[1] = total[:, HALF:2 * HALF]
    fin[2] = total[:, 2 * HALF:W3]

    to_partner = remote(fin.at[1 + c], fin_in.at[0], f_s.at[0], f_r.at[0], partner)
    to_partner.start()
    onward = remote(fin.at[2 * (1 - c)], fin_in.at[1 + c], f_s.at[1], f_r.at[1 + c], at(core=0, dzh=1))
    onward.start()
    loads[6].wait()
    to_partner.wait_recv()

    @pl.when(c == 0)
    def _():
        for i in range(2):
            remote(fin.at[0], fin_in.at[1 + i], f_s.at[1], f_r.at[1 + i], partner).wait_recv()
        got0 = jnp.where(zh == 0, 0.0, fin_in[1])
        got1 = jnp.where(zh == 0, 0.0, fin_in[2])
        out[0, :, 0:HALF] = fin[0] + got0 - tgt[:, 0:HALF]
        out[0, :, HALF:D] = fin_in[0] + got1 - tgt[:, HALF:D]

    @pl.when(c == 1)
    def _():
        out[0, :, 0:HALF] = fin_in[0] - tgt[:, 0:HALF]
        out[0, :, HALF:D] = fin[1] - tgt[:, HALF:D]

    to_partner.wait_send()
    onward.wait_send()
    for copy in sent:
        copy.wait_send()


def body(*args):
    f32, bf16 = jnp.float32, jnp.bfloat16
    dma = pltpu.SemaphoreType.DMA
    v = pltpu.VMEM
    return pl.pallas_call(
        kernel,
        out_shape=jax.ShapeDtypeStruct((1, 4, D), f32),
        in_specs=[pl.BlockSpec(memory_space=pl.ANY)] * 7,
        out_specs=pl.BlockSpec(memory_space=pltpu.VMEM),
        scratch_shapes=[
            v((4, D), f32),
            v((D, FEATS), bf16),
            v((1, FEATS), f32),
            v((1, FEATS), f32),
            v((4, D), f32),
            v((4, FEATS, HALF), bf16),
            v((NQ, 4, D), bf16),
            v((NH, HR, D), bf16),
            v((NH, HR, FEATS), bf16),
            v((NH, HR, FEATS), bf16),
            v((NH, HR, W3), f32),
            v((NH, 4, XR, MID), bf16),
            v((NH, 6, XR, MID), bf16),
            v((NH, 2, XR, MID), bf16),
            v((NQ, 4, W3), bf16),
            v((NQ, 4, W3), bf16),
            v((4, W3), f32),
            v((3, 4, HALF), f32),
            v((3, 4, HALF), f32),
            dma((7,)), dma((NQ,)), dma((NQ,)), dma((NH, 4)), dma((NH, 4)), dma((2,)), dma((2,)),
            dma((NH,)), dma((NH,)), dma((NH, 6)), dma((NH, 6)), dma((NQ,)), dma((NQ,)), dma((2,)), dma((3,)),
        ],
        compiler_params=pltpu.CompilerParams(
            collective_id=0, has_side_effects=True, vmem_limit_bytes=56 * 2**20
        ),
    )(*args)


def solution(mesh):
    return jax.shard_map(
        body,
        mesh=mesh,
        in_specs=(
            P("layer", "feat", None),
            P("layer", None, "feat"),
            P("layer", "feat"),
            P("layer", "feat"),
            P("layer", "feat", None),
            P("layer", "feat", None),
            P("layer", "feat", None),
        ),
        out_specs=P("layer", "feat", None),
        check_vma=False,
    )
```

```python
import jax
import jax.numpy as jnp
from jax import lax
from jax.experimental import pallas as pl
from jax.experimental.pallas import tpu as pltpu
from jax.sharding import PartitionSpec as P

MESH = pl.DeviceIdType.MESH
D = 2048
HALF = 1024
FEATS = 384
W3 = 3 * HALF
PIECES = (
    (4, 1), (4, 0), (3, 1), (-3, 1), (3, 0), (-3, 0), (-2, 1), (-2, 0),
    (2, 1), (1, 1), (-1, 1), (0, 1), (2, 0), (1, 0), (-1, 0), (0, 0),
)
NQ = 16
NH = 2
OWN = 15
PER = NQ // NH
XR = PER * 4
HR = 4 * XR
GROUP = 16
NG = 4
STAY = 2 * HALF
UNITS = ((1, STAY, W3, 0, XR), (0, STAY, W3, 0, XR), (0, 0, STAY, 0, XR), (1, 0, STAY, GROUP, XR))
GA = 1536
GB = D - GA
PIECES_B = ((2, 1), (2, 0), (1, 1), (3, 1), (1, 0), (3, 0), (0, 1), (0, 0))
OWN_B = 7


def kernel(
    source, w_enc, b_enc, threshold, dec_self, dec_next, target, out,
    rows, wv, bv, tv, tgt, dbuf, piece, pb, zxs, zxr, xa, cod, cod_o, acc,
    xs, xin, zs, zr, own, fin, fin_in,
    lsem, ag_s, ag_r, b1_s, b1_r, b2_s, b2_r, zx_s, zx_r, ax_s, ax_r, dw_s, dw_r, cx_s, cx_r, rx_s, rx_r, rz_s, rz_r, f_s, f_r,
):
    layer, feat = lax.axis_index("layer"), lax.axis_index("feat")
    zh, c = layer // 2, layer % 2
    x, y, z = feat // 16, (feat // 2) % 8, feat % 2

    def at(dx=0, dy=0, dz=0, core=None, dzh=0):
        core = c if core is None else core
        where = lax.rem(zh + dzh + 4, 4) * 2 + core
        place = lax.rem(x + dx + 4, 4) * 16 + lax.rem(y + dy + 8, 8) * 2
        return (where, place + (1 - z if dz else z))

    partner = at(core=1 - c)

    def remote(src, dst, send, recv, to):
        return pltpu.make_async_remote_copy(
            src_ref=src, dst_ref=dst, send_sem=send, recv_sem=recv, device_id=to, device_id_type=MESH
        )

    mine = pl.ds(pl.multiple_of(c * HALF, HALF), HALF)
    theirs = pl.ds(pl.multiple_of((1 - c) * HALF, HALF), HALF)
    loads = [
        pltpu.make_async_copy(source.at[0], rows, lsem.at[0]),
        pltpu.make_async_copy(w_enc.at[0], wv, lsem.at[1]),
        pltpu.make_async_copy(b_enc, bv, lsem.at[2]),
        pltpu.make_async_copy(threshold, tv, lsem.at[3]),
        pltpu.make_async_copy(dec_self.at[0, :, mine], dbuf.at[c], lsem.at[4]),
        pltpu.make_async_copy(dec_next.at[0, :, mine], dbuf.at[1 - c], lsem.at[5]),
        pltpu.make_async_copy(target.at[0], tgt, lsem.at[6]),
    ]
    for load in loads:
        load.start()

    barrier = pltpu.get_barrier_semaphore()
    peers = [at(dy=dy, dz=dz) for dy, dz in PIECES[:OWN]] + [partner]
    peers += [at(dx=dx, dz=dz) for dx, dz in PIECES_B if dx]
    peers += [at(dy=dy, dz=dz, dzh=-1) for dy, dz in PIECES]
    for peer in peers:
        pl.semaphore_signal(barrier, inc=1, device_id=peer, device_id_type=MESH)

    loads[0].wait()
    r = rows[...]
    scale = lax.rsqrt(jnp.mean(r * r, axis=1, keepdims=True) + 1e-05)
    normed = (r * scale).astype(jnp.bfloat16)
    piece[OWN] = normed[:, 0:GA]
    pb[0, OWN_B] = normed[:, GA:D]
    pl.semaphore_wait(barrier, len(peers))

    sent = []

    def go(copy):
        copy.start()
        sent.append(copy)
        return copy

    gather = [
        remote(piece.at[OWN], piece.at[q], ag_s.at[q], ag_r.at[q], at(dy=PIECES[q][0], dz=PIECES[q][1]))
        for q in range(OWN)
    ]
    gather_b = [
        remote(pb.at[0, OWN_B], pb.at[0, p], b1_s.at[p], b1_r.at[p], at(dx=PIECES_B[p][0], dz=PIECES_B[p][1]))
        for p in range(OWN_B)
    ]
    for q in reversed(range(OWN)):
        go(gather[q])
    for copy in gather_b:
        go(copy)
    lent = [
        remote(dec_self.at[0, :, theirs], dbuf.at[3 - c], dw_s.at[0], dw_r.at[0], partner),
        remote(dec_next.at[0, :, theirs], dbuf.at[2 + c], dw_s.at[1], dw_r.at[1], partner),
    ]
    for copy in lent:
        go(copy)

    spread = {}
    for g in reversed(range(NG)):
        for q in range(g * 4, g * 4 + 4):
            if q != OWN:
                gather[q].wait_recv()
        h, r0 = g // 2, (g % 2) * GROUP
        xa[h, r0:r0 + GROUP, 0:GA] = jnp.concatenate([piece[q] for q in range(g * 4, g * 4 + 4)], axis=0)
        block = xa.at[h, r0:r0 + GROUP, 0:GA]
        spread[g] = [
            go(remote(block, xa.at[h, pl.ds((4 - d) * XR + r0, GROUP), 0:GA], ax_s.at[g, d], ax_r.at[g, d], at(dx=d)))
            for d in (2, 1, 3)
        ]
        if g == NG - 1:
            for copy in gather_b:
                copy.wait_recv()
            spread_b = {
                dy: go(remote(pb.at[0], pb.at[8 - dy], b2_s.at[dy], b2_r.at[8 - dy], at(dy=dy)))
                for dy in (1, 7, 2, 6, 3, 5, 4)
            }

    def arrived(h):
        for g in (2 * h + 1, 2 * h):
            for copy in spread[g]:
                copy.wait_recv()
        for dy in {1: (2, 1, 7), 0: (3, 4, 5, 6)}[h]:
            spread_b[dy].wait_recv()
        for dx in range(4):
            for k in range(2):
                rows_b = []
                for q in range(h * PER + 4 * k, h * PER + 4 * k + 4):
                    dy, dz = PIECES[q]
                    rows_b.append(pb[-dy % 8, PIECES_B.index((-dx % 4, dz))])
                r0 = dx * XR + k * GROUP
                xa[h, r0:r0 + GROUP, GA:D] = jnp.concatenate(rows_b, axis=0)

    def encode(h):
        pre = jnp.dot(xa[h], wv[...], preferred_element_type=jnp.float32) + bv[...]
        cod[h] = (pre * jax.nn.sigmoid((pre - tv[...]) / 0.1)).astype(jnp.bfloat16)
        copy = remote(cod.at[h], cod_o.at[h], cx_s.at[h], cx_r.at[h], partner)
        return go(copy)

    def unit(u):
        h, lo, hi, r0, r1 = UNITS[u]
        return h, lo, (lo + hi) // 2, hi, r0, r1, (r1 - r0, (hi - lo) // 2)

    def toward(u, i, value, size):
        n, wide = size
        src = xs.at[u, i, 0:n, 0:wide]
        xs[u, i, 0:n, 0:wide] = value.astype(jnp.bfloat16)
        return go(remote(
            src, xin.at[u, i, 0:n, 0:wide], rx_s.at[u, i], rx_r.at[u, i], at(dx=1 if i % 2 == 0 else -1)
        ))

    def part(u, d, lo, hi):
        h, _, _, _, r0, r1, _ = unit(u)
        return acc[h, d * XR + r0:d * XR + r1, lo:hi]

    def scatter_far(u):
        h, lo, mid, hi, r0, r1, size = unit(u)
        return [toward(u, 0, part(u, 2, lo, mid), size), toward(u, 1, part(u, 2, mid, hi), size)]

    def scatter_near(u):
        h, lo, mid, hi, r0, r1, size = unit(u)
        return [toward(u, 2, part(u, 1, mid, hi), size), toward(u, 3, part(u, 3, lo, mid), size)]

    def came_x(u, i):
        n, wide = unit(u)[-1]
        return xin[u, i, 0:n, 0:wide].astype(jnp.float32)

    def relay_x(u, far):
        h, lo, mid, hi, r0, r1, size = unit(u)
        out_ = []
        for i, (d, p, e) in enumerate(((1, lo, mid), (3, mid, hi))):
            far[i].wait_recv()
            out_.append(toward(u, 4 + i, part(u, d, p, e) + came_x(u, i), size))
        return out_

    def scatter_zy(u, near, last):
        h, lo, mid, hi, r0, r1, size = unit(u)
        for copy in near + last:
            copy.wait_recv()
        left = part(u, 0, lo, mid) + (came_x(u, 4) + came_x(u, 3))
        right = part(u, 0, mid, hi) + (came_x(u, 2) + came_x(u, 5))
        copies = []
        for i in range((r1 - r0) // 4):
            q = h * PER + r0 // 4 + i
            if q == OWN and lo == 0:
                own[:, lo:mid] = left[4 * i:4 * i + 4]
                own[:, mid:hi] = right[4 * i:4 * i + 4]
                continue
            zs[q, :, lo:mid] = left[4 * i:4 * i + 4].astype(jnp.bfloat16)
            zs[q, :, mid:hi] = right[4 * i:4 * i + 4].astype(jnp.bfloat16)
            dy, dz = PIECES[q]
            kind = 0 if lo == 0 else 1
            copies.append(go(remote(
                zs.at[q, :, lo:hi], zr.at[q, :, lo:hi], rz_s.at[kind, q], rz_r.at[kind, q],
                at(dy=-dy, dz=dz, dzh=kind),
            )))
        return copies

    def z_send(dx):
        zxs[dx] = acc[1, dx * XR:dx * XR + GROUP, 0:STAY].astype(jnp.bfloat16)
        return go(remote(zxs.at[dx], zxr.at[dx], zx_s.at[dx], zx_r.at[dx], at(dz=1)))

    def z_add(dx):
        zx[dx].wait_recv()
        acc[1, dx * XR + GROUP:(dx + 1) * XR, 0:STAY] += zxr[dx].astype(jnp.float32)

    first = pl.ds(pl.multiple_of(c * STAY, HALF), HALF)
    other = pl.ds(pl.multiple_of((1 - c) * STAY, HALF), HALF)

    def decode_own(h):
        acc[h, :, first] = jnp.dot(cod[h], dbuf[0], preferred_element_type=jnp.float32)
        acc[h, :, HALF:STAY] = jnp.dot(cod[h], dbuf[1], preferred_element_type=jnp.float32)

    def decode_other(h):
        codes[h].wait_recv()
        acc[h, :, other] = jnp.dot(cod_o[h], dbuf[3], preferred_element_type=jnp.float32)
        acc[h, :, HALF:STAY] += jnp.dot(cod_o[h], dbuf[2], preferred_element_type=jnp.float32)

    codes = {}
    for i in (1, 2, 3):
        loads[i].wait()
    arrived(1)
    codes[1] = encode(1)
    loads[4].wait()
    loads[5].wait()
    decode_own(1)
    for copy in lent:
        copy.wait_recv()
    decode_other(1)
    far, near, last, zy = {}, {}, {}, {}
    far[0] = scatter_far(0)
    near[0] = scatter_near(0)
    zx = {dx: z_send(dx) for dx in (2, 1, 3, 0)}
    arrived(0)
    codes[0] = encode(0)
    decode_own(0)
    decode_other(0)
    far[1] = scatter_far(1)
    near[1] = scatter_near(1)
    far[2] = scatter_far(2)
    last[0] = relay_x(0, far[0])
    near[2] = scatter_near(2)
    last[1] = relay_x(1, far[1])
    z_add(2)
    far[3] = scatter_far(3)
    last[2] = relay_x(2, far[2])
    z_add(1)
    z_add(3)
    near[3] = scatter_near(3)
    zy[0] = scatter_zy(0, near[0], last[0])
    zy[1] = scatter_zy(1, near[1], last[1])
    last[3] = relay_x(3, far[3])
    z_add(0)
    zy[2] = scatter_zy(2, near[2], last[2])
    zy[3] = scatter_zy(3, near[3], last[3])

    def gathered(total, copies, u):
        h, lo, hi, r0, r1 = UNITS[u]
        for copy in copies:
            copy.wait_recv()
        for q in range(h * PER + r0 // 4, h * PER + r1 // 4):
            if q != OWN or lo:
                total = total + zr[q, :, lo:hi].astype(jnp.float32)
        return total

    stay = gathered(own[...], zy[2], 2)
    came = gathered(jnp.zeros((4, HALF), jnp.float32), zy[0], 0)
    came = gathered(came, zy[1], 1)
    stay = gathered(stay, zy[3], 3)
    fin[0] = stay[:, 0:HALF] + jnp.where(zh == 0, 0.0, came)
    fin[1] = stay[:, HALF:STAY]
    loads[6].wait()
    swap = remote(fin.at[1 - c], fin_in.at[0], f_s.at[0], f_r.at[0], partner)
    swap.start()
    out[0, :, mine] = fin[c] - tgt[:, mine]
    swap.wait_recv()
    out[0, :, theirs] = fin_in[0] - tgt[:, theirs]
    swap.wait_send()
    for copy in sent:
        copy.wait_send()


def body(*args):
    f32, bf16 = jnp.float32, jnp.bfloat16
    dma = pltpu.SemaphoreType.DMA
    v = pltpu.VMEM
    return pl.pallas_call(
        kernel,
        out_shape=jax.ShapeDtypeStruct((1, 4, D), f32),
        in_specs=[pl.BlockSpec(memory_space=pl.ANY)] * 7,
        out_specs=pl.BlockSpec(memory_space=pltpu.VMEM),
        scratch_shapes=[
            v((4, D), f32),
            v((D, FEATS), bf16),
            v((1, FEATS), f32),
            v((1, FEATS), f32),
            v((4, D), f32),
            v((4, FEATS, HALF), bf16),
            v((NQ, 4, GA), bf16),
            v((8, 8, 4, GB), bf16),
            v((4, GROUP, STAY), bf16),
            v((4, GROUP, STAY), bf16),
            v((NH, HR, D), bf16),
            v((NH, HR, FEATS), bf16),
            v((NH, HR, FEATS), bf16),
            v((NH, HR, W3), f32),
            v((4, 6, XR, HALF), bf16),
            v((4, 6, XR, HALF), bf16),
            v((NQ, 4, W3), bf16),
            v((NQ, 4, W3), bf16),
            v((4, STAY), f32),
            v((2, 4, HALF), f32),
            v((1, 4, HALF), f32),
            dma((7,)), dma((NQ,)), dma((NQ,)), dma((8,)), dma((8,)), dma((8,)), dma((8,)), dma((4,)), dma((4,)), dma((NG, 4)), dma((NG, 4)), dma((2,)), dma((2,)),
            dma((NH,)), dma((NH,)), dma((4, 6)), dma((4, 6)), dma((2, NQ)), dma((2, NQ)), dma((1,)), dma((1,)),
        ],
        compiler_params=pltpu.CompilerParams(
            collective_id=0, has_side_effects=True, vmem_limit_bytes=56 * 2**20
        ),
    )(*args)


def solution(mesh):
    return jax.shard_map(
        body,
        mesh=mesh,
        in_specs=(
            P("layer", "feat", None),
            P("layer", None, "feat"),
            P("layer", "feat"),
            P("layer", "feat"),
            P("layer", "feat", None),
            P("layer", "feat", None),
            P("layer", "feat", None),
        ),
        out_specs=P("layer", "feat", None),
        check_vma=False,
    )
```

```python
import jax
import jax.numpy as jnp
from jax import lax
from jax.experimental import pallas as pl
from jax.experimental.pallas import tpu as pltpu
from jax.sharding import PartitionSpec as P

MESH = pl.DeviceIdType.MESH
D = 2048
HALF = 1024
FEATS = 384
W3 = 3 * HALF
PIECES = (
    (4, 1), (4, 0), (3, 1), (-3, 1), (3, 0), (-3, 0), (-2, 1), (-2, 0),
    (2, 1), (1, 1), (-1, 1), (0, 1), (2, 0), (1, 0), (-1, 0), (0, 0),
)
NQ = 16
NH = 2
OWN = 15
PER = NQ // NH
XR = PER * 4
HR = 4 * XR
GROUP = 16
NG = 4
STAY = 2 * HALF
UNITS = ((1, STAY, W3, 0, XR), (0, STAY, W3, 0, XR), (0, 0, STAY, 0, XR), (1, 0, STAY, GROUP, XR))
GA = 1536
GB = D - GA
PIECES_B = ((2, 1), (2, 0), (1, 1), (3, 1), (1, 0), (3, 0), (0, 1), (0, 0))
OWN_B = 7


def kernel(
    source, w_enc, b_enc, threshold, dec_self, dec_next, target, out,
    rows, wv, bv, tv, tgt, dbuf, piece, pb, zxs, zxr, xa, cod, cod_o, acc,
    xs, xin, zs, zr, own, fin, fin_in,
    lsem, ag_s, ag_r, b1_s, b1_r, b2_s, b2_r, zx_s, zx_r, ax_s, ax_r, dw_s, dw_r, cx_s, cx_r, rx_s, rx_r, rz_s, rz_r, f_s, f_r,
):
    layer, feat = lax.axis_index("layer"), lax.axis_index("feat")
    zh, c = layer // 2, layer % 2
    x, y, z = feat // 16, (feat // 2) % 8, feat % 2

    def at(dx=0, dy=0, dz=0, core=None, dzh=0):
        core = c if core is None else core
        where = lax.rem(zh + dzh + 4, 4) * 2 + core
        place = lax.rem(x + dx + 4, 4) * 16 + lax.rem(y + dy + 8, 8) * 2
        return (where, place + (1 - z if dz else z))

    partner = at(core=1 - c)

    def remote(src, dst, send, recv, to):
        return pltpu.make_async_remote_copy(
            src_ref=src, dst_ref=dst, send_sem=send, recv_sem=recv, device_id=to, device_id_type=MESH
        )

    mine = pl.ds(pl.multiple_of(c * HALF, HALF), HALF)
    theirs = pl.ds(pl.multiple_of((1 - c) * HALF, HALF), HALF)
    loads = [
        pltpu.make_async_copy(source.at[0], rows, lsem.at[0]),
        pltpu.make_async_copy(w_enc.at[0], wv, lsem.at[1]),
        pltpu.make_async_copy(b_enc, bv, lsem.at[2]),
        pltpu.make_async_copy(threshold, tv, lsem.at[3]),
        pltpu.make_async_copy(dec_self.at[0, :, mine], dbuf.at[c], lsem.at[4]),
        pltpu.make_async_copy(dec_next.at[0, :, mine], dbuf.at[1 - c], lsem.at[5]),
        pltpu.make_async_copy(target.at[0], tgt, lsem.at[6]),
    ]
    for load in loads:
        load.start()

    barrier = pltpu.get_barrier_semaphore()
    peers = [at(dy=dy, dz=dz) for dy, dz in PIECES[:OWN]] + [partner]
    peers += [at(dx=dx, dz=dz) for dx, dz in PIECES_B if dx]
    peers += [at(dy=dy, dz=dz, dzh=-1) for dy, dz in PIECES]
    for peer in peers:
        pl.semaphore_signal(barrier, inc=1, device_id=peer, device_id_type=MESH)

    loads[0].wait()
    r = rows[...]
    scale = lax.rsqrt(jnp.mean(r * r, axis=1, keepdims=True) + 1e-05)
    normed = (r * scale).astype(jnp.bfloat16)
    piece[OWN] = normed[:, 0:GA]
    pb[0, OWN_B] = normed[:, GA:D]
    pl.semaphore_wait(barrier, len(peers))

    def go(copy):
        copy.start()
        return copy

    def take(ref, sem):
        pltpu.make_async_copy(ref, ref, sem).wait()

    direct = range(OWN)
    gather = {
        q: remote(piece.at[OWN], piece.at[q], ag_s.at[0], ag_r.at[q // 4], at(dy=PIECES[q][0], dz=PIECES[q][1]))
        for q in direct
    }
    gather_b = [
        remote(pb.at[0, OWN_B], pb.at[0, p], b1_s.at[0], b1_r.at[0], at(dx=PIECES_B[p][0], dz=PIECES_B[p][1]))
        for p in range(OWN_B)
    ]
    for q in reversed(direct):
        go(gather[q])
    for copy in gather_b:
        go(copy)
    lent = [
        remote(dec_self.at[0, :, theirs], dbuf.at[3 - c], dw_s.at[0], dw_r.at[0], partner),
        remote(dec_next.at[0, :, theirs], dbuf.at[2 + c], dw_s.at[0], dw_r.at[0], partner),
    ]
    for copy in lent:
        go(copy)

    for g in (3, 2, 1, 0):
        take(piece.at[4 * g:min(4 * g + 4, OWN)], ag_r.at[g])
        h, r0 = g // 2, (g % 2) * GROUP
        xa[h, r0:r0 + GROUP, 0:GA] = jnp.concatenate([piece[q] for q in range(g * 4, g * 4 + 4)], axis=0)
        block = xa.at[h, r0:r0 + GROUP, 0:GA]
        for d in (2, 1, 3):
            go(remote(block, xa.at[h, pl.ds((4 - d) * XR + r0, GROUP), 0:GA], ax_s.at[0], ax_r.at[h], at(dx=d)))
        if g == NG - 1:
            take(pb.at[0, 0:OWN_B], b1_r.at[0])
            for dy in (1, 7, 2, 6, 3, 5, 4):
                there = 8 - dy
                end = b2_r.at[0 if there in (2, 3, 4, 5) else 1]
                go(remote(pb.at[0], pb.at[there], b2_s.at[0], end, at(dy=dy)))

    def arrived(h):
        take(pb.at[0:3] if h else pb.at[3:7], b2_r.at[h])
        for dx in range(4):
            for k in range(2):
                rows_b = []
                for q in range(h * PER + 4 * k, h * PER + 4 * k + 4):
                    dy, dz = PIECES[q]
                    rows_b.append(pb[-dy % 8, PIECES_B.index((-dx % 4, dz))])
                r0 = dx * XR + k * GROUP
                xa[h, r0:r0 + GROUP, GA:D] = jnp.concatenate(rows_b, axis=0)
        take(xa.at[h, 0:3 * XR, 0:GA], ax_r.at[h])

    def encode(h):
        pre = jnp.dot(xa[h], wv[...], preferred_element_type=jnp.float32) + bv[...]
        cod[h] = (pre * jax.nn.sigmoid((pre - tv[...]) / 0.1)).astype(jnp.bfloat16)
        copy = remote(cod.at[h], cod_o.at[h], cx_s.at[h], cx_r.at[h], partner)
        return go(copy)

    def unit(u):
        h, lo, hi, r0, r1 = UNITS[u]
        return h, lo, (lo + hi) // 2, hi, r0, r1, (r1 - r0, (hi - lo) // 2)

    def toward(u, i, value, size):
        n, wide = size
        src = xs.at[u, i, 0:n, 0:wide]
        xs[u, i, 0:n, 0:wide] = value.astype(jnp.bfloat16)
        return go(remote(
            src, xin.at[u, i, 0:n, 0:wide], rx_s.at[u], rx_r.at[u, min(i, 2)], at(dx=1 if i % 2 == 0 else -1)
        ))

    def part(u, d, lo, hi):
        h, _, _, _, r0, r1, _ = unit(u)
        return acc[h, d * XR + r0:d * XR + r1, lo:hi]

    def scatter_far(u):
        h, lo, mid, hi, r0, r1, size = unit(u)
        return [toward(u, 0, part(u, 2, lo, mid), size), toward(u, 1, part(u, 2, mid, hi), size)]

    def scatter_near(u):
        h, lo, mid, hi, r0, r1, size = unit(u)
        toward(u, 2, part(u, 1, mid, hi), size)
        toward(u, 3, part(u, 3, lo, mid), size)

    def came_x(u, i):
        n, wide = unit(u)[-1]
        return xin[u, i, 0:n, 0:wide].astype(jnp.float32)

    def relay_x(u, far):
        h, lo, mid, hi, r0, r1, size = unit(u)
        for i, (d, p, e) in enumerate(((1, lo, mid), (3, mid, hi))):
            far[i].wait_recv()
            toward(u, 4 + i, part(u, d, p, e) + came_x(u, i), size)

    def scatter_zy(u):
        h, lo, mid, hi, r0, r1, size = unit(u)
        take(xin.at[u, 2:6, 0:size[0], 0:size[1]], rx_r.at[u, 2])
        left = part(u, 0, lo, mid) + (came_x(u, 4) + came_x(u, 3))
        right = part(u, 0, mid, hi) + (came_x(u, 2) + came_x(u, 5))
        for i in range((r1 - r0) // 4):
            q = h * PER + r0 // 4 + i
            if q == OWN and lo == 0:
                own[:, lo:mid] = left[4 * i:4 * i + 4]
                own[:, mid:hi] = right[4 * i:4 * i + 4]
                continue
            zs[q, :, lo:mid] = left[4 * i:4 * i + 4].astype(jnp.bfloat16)
            zs[q, :, mid:hi] = right[4 * i:4 * i + 4].astype(jnp.bfloat16)
            dy, dz = PIECES[q]
            kind = 0 if lo == 0 else 1
            go(remote(
                zs.at[q, :, lo:hi], zr.at[q, :, lo:hi], rz_s.at[u], rz_r.at[u],
                at(dy=-dy, dz=dz, dzh=kind),
            ))

    def z_send(dx):
        zxs[dx] = acc[1, dx * XR:dx * XR + GROUP, 0:STAY].astype(jnp.bfloat16)
        return go(remote(zxs.at[dx], zxr.at[dx], zx_s.at[0], zx_r.at[dx], at(dz=1)))

    def z_add(dx):
        zx[dx].wait_recv()
        acc[1, dx * XR + GROUP:(dx + 1) * XR, 0:STAY] += zxr[dx].astype(jnp.float32)

    first = pl.ds(pl.multiple_of(c * STAY, HALF), HALF)
    other = pl.ds(pl.multiple_of((1 - c) * STAY, HALF), HALF)

    def decode_own(h):
        acc[h, :, first] = jnp.dot(cod[h], dbuf[0], preferred_element_type=jnp.float32)
        acc[h, :, HALF:STAY] = jnp.dot(cod[h], dbuf[1], preferred_element_type=jnp.float32)

    def decode_other(h):
        codes[h].wait_recv()
        acc[h, :, other] = jnp.dot(cod_o[h], dbuf[3], preferred_element_type=jnp.float32)

    def decode_mixed(h):
        acc[h, :, HALF:STAY] += jnp.dot(cod_o[h], dbuf[2], preferred_element_type=jnp.float32)

    codes = {}
    for i in (1, 2, 3):
        loads[i].wait()
    far, zx = {}, {}
    arrived(1)
    codes[1] = encode(1)
    loads[4].wait()
    loads[5].wait()
    decode_own(1)
    take(dbuf.at[0:2], dw_r.at[0])
    decode_other(1)
    far[0] = scatter_far(0)
    scatter_near(0)
    decode_mixed(1)
    for dx in (2, 1, 3, 0):
        zx[dx] = z_send(dx)
    arrived(0)
    codes[0] = encode(0)
    decode_own(0)
    decode_other(0)
    far[1] = scatter_far(1)
    scatter_near(1)
    decode_mixed(0)
    far[2] = scatter_far(2)
    relay_x(0, far[0])
    scatter_near(2)
    relay_x(1, far[1])
    scatter_zy(0)
    z_add(2)
    far[3] = scatter_far(3)
    relay_x(2, far[2])
    z_add(1)
    z_add(3)
    scatter_near(3)
    scatter_zy(1)
    relay_x(3, far[3])
    scatter_zy(2)
    z_add(0)
    scatter_zy(3)
    take(piece.at[0:OWN], ag_s.at[0])
    take(pb.at[0, 0:OWN_B], b1_s.at[0])
    take(pb.at[0:7], b2_s.at[0])
    take(xa.at[:, 0:3 * XR, 0:GA], ax_s.at[0])
    take(dbuf.at[0:2], dw_s.at[0])
    take(zxs, zx_s.at[0])
    for h in range(NH):
        codes[h].wait_send()

    def gathered(total, u):
        h, lo, hi, r0, r1 = UNITS[u]
        q0, q1 = h * PER + r0 // 4, h * PER + r1 // 4
        take(zr.at[q0:min(q1, OWN) if lo == 0 else q1, :, lo:hi], rz_r.at[u])
        for q in range(h * PER + r0 // 4, h * PER + r1 // 4):
            if q != OWN or lo:
                total = total + zr[q, :, lo:hi].astype(jnp.float32)
        return total

    came = gathered(jnp.zeros((4, HALF), jnp.float32), 0)
    came = gathered(came, 1)
    stay = gathered(own[...], 3)
    stay = gathered(stay, 2)
    fin[0] = stay[:, 0:HALF] + jnp.where(zh == 0, 0.0, came)
    fin[1] = stay[:, HALF:STAY]
    loads[6].wait()
    swap = remote(fin.at[1 - c], fin_in.at[0], f_s.at[0], f_r.at[0], partner)
    swap.start()
    out[0, :, mine] = fin[c] - tgt[:, mine]
    swap.wait_recv()
    out[0, :, theirs] = fin_in[0] - tgt[:, theirs]
    swap.wait_send()
    for u in range(4):
        h, lo, mid, hi, r0, r1, (n, wide) = unit(u)
        q0, q1 = h * PER + r0 // 4, h * PER + r1 // 4
        take(xs.at[u, :, 0:n, 0:wide], rx_s.at[u])
        take(zs.at[q0:min(q1, OWN) if lo == 0 else q1, :, lo:hi], rz_s.at[u])


def body(*args):
    f32, bf16 = jnp.float32, jnp.bfloat16
    dma = pltpu.SemaphoreType.DMA
    v = pltpu.VMEM
    return pl.pallas_call(
        kernel,
        out_shape=jax.ShapeDtypeStruct((1, 4, D), f32),
        in_specs=[pl.BlockSpec(memory_space=pl.ANY)] * 7,
        out_specs=pl.BlockSpec(memory_space=pltpu.VMEM),
        scratch_shapes=[
            v((4, D), f32),
            v((D, FEATS), bf16),
            v((1, FEATS), f32),
            v((1, FEATS), f32),
            v((4, D), f32),
            v((4, FEATS, HALF), bf16),
            v((NQ, 4, GA), bf16),
            v((8, 8, 4, GB), bf16),
            v((4, GROUP, STAY), bf16),
            v((4, GROUP, STAY), bf16),
            v((NH, HR, D), bf16),
            v((NH, HR, FEATS), bf16),
            v((NH, HR, FEATS), bf16),
            v((NH, HR, W3), f32),
            v((4, 6, XR, HALF), bf16),
            v((4, 6, XR, HALF), bf16),
            v((NQ, 4, W3), bf16),
            v((NQ, 4, W3), bf16),
            v((4, STAY), f32),
            v((2, 4, HALF), f32),
            v((1, 4, HALF), f32),
            dma((7,)), dma((1,)), dma((NG,)), dma((1,)), dma((1,)), dma((1,)), dma((NH,)), dma((1,)), dma((4,)),
            dma((1,)), dma((NH,)), dma((1,)), dma((1,)), dma((NH,)), dma((NH,)), dma((4,)), dma((4, 3)),
            dma((4,)), dma((4,)), dma((1,)), dma((1,)),
        ],
        compiler_params=pltpu.CompilerParams(
            collective_id=0, has_side_effects=True, vmem_limit_bytes=56 * 2**20
        ),
    )(*args)


def solution(mesh):
    return jax.shard_map(
        body,
        mesh=mesh,
        in_specs=(
            P("layer", "feat", None),
            P("layer", None, "feat"),
            P("layer", "feat"),
            P("layer", "feat"),
            P("layer", "feat", None),
            P("layer", "feat", None),
            P("layer", "feat", None),
        ),
        out_specs=P("layer", "feat", None),
        check_vma=False,
    )
```

```python
import jax
import jax.numpy as jnp
from jax import lax
from jax.experimental import pallas as pl
from jax.experimental.pallas import tpu as pltpu
from jax.sharding import PartitionSpec as P

MESH = pl.DeviceIdType.MESH
D = 2048
HALF = 1024
FEATS = 384
W3 = 3 * HALF
PIECES = (
    (4, 1), (4, 0), (3, 1), (-3, 1), (3, 0), (-3, 0), (-2, 1), (-2, 0),
    (2, 1), (1, 1), (-1, 1), (0, 1), (2, 0), (1, 0), (-1, 0), (0, 0),
)
NQ = 16
NH = 2
OWN = 15
PER = NQ // NH
XR = PER * 4
HR = 4 * XR
GROUP = 16
NG = 4
STAY = 2 * HALF
UNITS = ((1, STAY, W3, 0, XR), (0, STAY, W3, 0, XR), (0, 0, STAY, 0, XR), (1, 0, STAY, GROUP, XR))
GA = 1536
GB = D - GA
PIECES_B = ((2, 1), (2, 0), (1, 1), (3, 1), (1, 0), (3, 0), (0, 1), (0, 0))
OWN_B = 7


def kernel(
    source, w_enc, b_enc, threshold, dec_self, dec_next, target, out,
    rows, wv, bv, tv, tgt, dbuf, piece, pb, zxs, zxr, xa, cod, cod_o, acc,
    xs, xin, zs, zr, own, fin, fin_in,
    lsem, ag_s, ag_r, b1_s, b1_r, b2_s, b2_r, zx_s, zx_r, ax_s, ax_r, dw_s, dw_r, cx_s, cx_r, rx_s, rx_r, rz_s, rz_r, f_s, f_r,
):
    layer, feat = lax.axis_index("layer"), lax.axis_index("feat")
    zh, c = layer // 2, layer % 2
    x, y, z = feat // 16, (feat // 2) % 8, feat % 2

    def at(dx=0, dy=0, dz=0, core=None, dzh=0):
        core = c if core is None else core
        where = lax.rem(zh + dzh + 4, 4) * 2 + core
        place = lax.rem(x + dx + 4, 4) * 16 + lax.rem(y + dy + 8, 8) * 2
        return (where, place + (1 - z if dz else z))

    partner = at(core=1 - c)

    def remote(src, dst, send, recv, to):
        return pltpu.make_async_remote_copy(
            src_ref=src, dst_ref=dst, send_sem=send, recv_sem=recv, device_id=to, device_id_type=MESH
        )

    mine = pl.ds(pl.multiple_of(c * HALF, HALF), HALF)
    theirs = pl.ds(pl.multiple_of((1 - c) * HALF, HALF), HALF)
    loads = [
        pltpu.make_async_copy(source.at[0], rows, lsem.at[0]),
        pltpu.make_async_copy(w_enc.at[0], wv, lsem.at[1]),
        pltpu.make_async_copy(b_enc, bv, lsem.at[2]),
        pltpu.make_async_copy(threshold, tv, lsem.at[3]),
        pltpu.make_async_copy(dec_self.at[0, :, mine], dbuf.at[c], lsem.at[4]),
        pltpu.make_async_copy(dec_next.at[0, :, mine], dbuf.at[1 - c], lsem.at[4]),
        pltpu.make_async_copy(target.at[0], tgt, lsem.at[5]),
    ]
    for load in loads:
        load.start()

    barrier = pltpu.get_barrier_semaphore()
    peers = [at(dy=dy, dz=dz) for dy, dz in PIECES[:OWN]] + [partner]
    peers += [at(dx=dx, dz=dz) for dx, dz in PIECES_B if dx]
    peers += [at(dy=dy, dz=dz, dzh=-1) for dy, dz in PIECES]
    for peer in peers:
        pl.semaphore_signal(barrier, inc=1, device_id=peer, device_id_type=MESH)

    loads[0].wait()
    r = rows[...]
    scale = lax.rsqrt(jnp.mean(r * r, axis=1, keepdims=True) + 1e-05)
    normed = (r * scale).astype(jnp.bfloat16)
    piece[OWN] = normed[:, 0:GA]
    pb[0, OWN_B] = normed[:, GA:D]
    pl.semaphore_wait(barrier, len(peers))

    def go(copy):
        copy.start()
        return copy

    def take(ref, sem):
        pltpu.make_async_copy(ref, ref, sem).wait()

    direct = range(OWN)
    gather = {
        q: remote(piece.at[OWN], piece.at[q], ag_s.at[0], ag_r.at[q // 4], at(dy=PIECES[q][0], dz=PIECES[q][1]))
        for q in direct
    }
    gather_b = [
        remote(pb.at[0, OWN_B], pb.at[0, p], b1_s.at[0], b1_r.at[0], at(dx=PIECES_B[p][0], dz=PIECES_B[p][1]))
        for p in range(OWN_B)
    ]
    for q in reversed(direct):
        go(gather[q])
    for copy in gather_b:
        go(copy)
    lent = [
        remote(dec_self.at[0, :, theirs], dbuf.at[3 - c], dw_s.at[0], dw_r.at[0], partner),
        remote(dec_next.at[0, :, theirs], dbuf.at[2 + c], dw_s.at[0], dw_r.at[0], partner),
    ]
    for copy in lent:
        go(copy)

    for g in (3, 2, 1, 0):
        take(piece.at[4 * g:min(4 * g + 4, OWN)], ag_r.at[g])
        h, r0 = g // 2, (g % 2) * GROUP
        xa[h, r0:r0 + GROUP, 0:GA] = jnp.concatenate([piece[q] for q in range(g * 4, g * 4 + 4)], axis=0)
        block = xa.at[h, r0:r0 + GROUP, 0:GA]
        for d in (2, 1, 3):
            go(remote(block, xa.at[h, pl.ds((4 - d) * XR + r0, GROUP), 0:GA], ax_s.at[0], ax_r.at[h], at(dx=d)))
        if g == NG - 1:
            take(pb.at[0, 0:OWN_B], b1_r.at[0])
            for dy in (1, 7, 2, 6, 3, 5, 4):
                there = 8 - dy
                end = b2_r.at[0 if there in (2, 3, 4, 5) else 1]
                go(remote(pb.at[0], pb.at[there], b2_s.at[0], end, at(dy=dy)))

    def arrived(h):
        take(pb.at[0:3] if h else pb.at[3:7], b2_r.at[h])
        for dx in range(4):
            for k in range(2):
                rows_b = []
                for q in range(h * PER + 4 * k, h * PER + 4 * k + 4):
                    dy, dz = PIECES[q]
                    rows_b.append(pb[-dy % 8, PIECES_B.index((-dx % 4, dz))])
                r0 = dx * XR + k * GROUP
                xa[h, r0:r0 + GROUP, GA:D] = jnp.concatenate(rows_b, axis=0)
        take(xa.at[h, 0:3 * XR, 0:GA], ax_r.at[h])

    def encode(h):
        pre = jnp.dot(xa[h], wv[...], preferred_element_type=jnp.float32) + bv[...]
        cod[h] = (pre * jax.nn.sigmoid((pre - tv[...]) / 0.1)).astype(jnp.bfloat16)
        copy = remote(cod.at[h], cod_o.at[h], cx_s.at[0], cx_r.at[h], partner)
        return go(copy)

    def unit(u):
        h, lo, hi, r0, r1 = UNITS[u]
        return h, lo, (lo + hi) // 2, hi, r0, r1, (r1 - r0, (hi - lo) // 2)

    def toward(u, i, value, size):
        n, wide = size
        src = xs.at[u, i, 0:n, 0:wide]
        xs[u, i, 0:n, 0:wide] = value.astype(jnp.bfloat16)
        return go(remote(
            src, xin.at[u, i, 0:n, 0:wide], rx_s.at[u], rx_r.at[u, min(i, 2)], at(dx=1 if i % 2 == 0 else -1)
        ))

    def part(u, d, lo, hi):
        h, _, _, _, r0, r1, _ = unit(u)
        return acc[h, d * XR + r0:d * XR + r1, lo:hi]

    def scatter_far(u):
        h, lo, mid, hi, r0, r1, size = unit(u)
        return [toward(u, 0, part(u, 2, lo, mid), size), toward(u, 1, part(u, 2, mid, hi), size)]

    def scatter_near(u):
        h, lo, mid, hi, r0, r1, size = unit(u)
        toward(u, 2, part(u, 1, mid, hi), size)
        toward(u, 3, part(u, 3, lo, mid), size)

    def came_x(u, i):
        n, wide = unit(u)[-1]
        return xin[u, i, 0:n, 0:wide].astype(jnp.float32)

    def relay_x(u, far):
        h, lo, mid, hi, r0, r1, size = unit(u)
        for i, (d, p, e) in enumerate(((1, lo, mid), (3, mid, hi))):
            far[i].wait_recv()
            toward(u, 4 + i, part(u, d, p, e) + came_x(u, i), size)

    def scatter_zy(u):
        h, lo, mid, hi, r0, r1, size = unit(u)
        take(xin.at[u, 2:6, 0:size[0], 0:size[1]], rx_r.at[u, 2])
        left = part(u, 0, lo, mid) + (came_x(u, 4) + came_x(u, 3))
        right = part(u, 0, mid, hi) + (came_x(u, 2) + came_x(u, 5))
        for i in range((r1 - r0) // 4):
            q = h * PER + r0 // 4 + i
            if q == OWN and lo == 0:
                own[:, lo:mid] = left[4 * i:4 * i + 4]
                own[:, mid:hi] = right[4 * i:4 * i + 4]
                continue
            zs[q, :, lo:mid] = left[4 * i:4 * i + 4].astype(jnp.bfloat16)
            zs[q, :, mid:hi] = right[4 * i:4 * i + 4].astype(jnp.bfloat16)
            dy, dz = PIECES[q]
            kind = 0 if lo == 0 else 1
            go(remote(
                zs.at[q, :, lo:hi], zr.at[q, :, lo:hi], rz_s.at[u], rz_r.at[u],
                at(dy=-dy, dz=dz, dzh=kind),
            ))

    def z_send(dx):
        zxs[dx] = acc[1, dx * XR:dx * XR + GROUP, 0:STAY].astype(jnp.bfloat16)
        return go(remote(zxs.at[dx], zxr.at[dx], zx_s.at[0], zx_r.at[dx], at(dz=1)))

    def z_add(dx):
        zx[dx].wait_recv()
        acc[1, dx * XR + GROUP:(dx + 1) * XR, 0:STAY] += zxr[dx].astype(jnp.float32)

    first = pl.ds(pl.multiple_of(c * STAY, HALF), HALF)
    other = pl.ds(pl.multiple_of((1 - c) * STAY, HALF), HALF)

    def decode_own(h):
        acc[h, :, first] = jnp.dot(cod[h], dbuf[0], preferred_element_type=jnp.float32)
        acc[h, :, HALF:STAY] = jnp.dot(cod[h], dbuf[1], preferred_element_type=jnp.float32)

    def decode_other(h):
        codes[h].wait_recv()
        acc[h, :, other] = jnp.dot(cod_o[h], dbuf[3], preferred_element_type=jnp.float32)

    def decode_mixed(h):
        acc[h, :, HALF:STAY] += jnp.dot(cod_o[h], dbuf[2], preferred_element_type=jnp.float32)

    codes = {}
    for i in (1, 2, 3):
        loads[i].wait()
    far, zx = {}, {}
    arrived(1)
    codes[1] = encode(1)
    take(dbuf.at[0:2], lsem.at[4])
    decode_own(1)
    take(dbuf.at[0:2], dw_r.at[0])
    decode_other(1)
    far[0] = scatter_far(0)
    scatter_near(0)
    decode_mixed(1)
    for dx in (2, 1, 3, 0):
        zx[dx] = z_send(dx)
    arrived(0)
    codes[0] = encode(0)
    decode_own(0)
    decode_other(0)
    far[1] = scatter_far(1)
    scatter_near(1)
    decode_mixed(0)
    far[2] = scatter_far(2)
    scatter_near(2)
    relay_x(0, far[0])
    relay_x(1, far[1])
    scatter_zy(0)
    z_add(2)
    far[3] = scatter_far(3)
    relay_x(2, far[2])
    z_add(1)
    z_add(3)
    scatter_near(3)
    scatter_zy(1)
    relay_x(3, far[3])
    scatter_zy(2)
    z_add(0)
    scatter_zy(3)
    take(piece.at[0:OWN], ag_s.at[0])
    take(pb.at[0, 0:OWN_B], b1_s.at[0])
    take(pb.at[0:7], b2_s.at[0])
    take(xa.at[:, 0:3 * XR, 0:GA], ax_s.at[0])
    take(dbuf.at[0:2], dw_s.at[0])
    take(zxs, zx_s.at[0])
    take(cod, cx_s.at[0])

    def gathered(total, u):
        h, lo, hi, r0, r1 = UNITS[u]
        q0, q1 = h * PER + r0 // 4, h * PER + r1 // 4
        take(zr.at[q0:min(q1, OWN) if lo == 0 else q1, :, lo:hi], rz_r.at[u])
        for q in range(h * PER + r0 // 4, h * PER + r1 // 4):
            if q != OWN or lo:
                total = total + zr[q, :, lo:hi].astype(jnp.float32)
        return total

    came = gathered(jnp.zeros((4, HALF), jnp.float32), 0)
    came = gathered(came, 1)
    stay = gathered(own[...], 3)
    stay = gathered(stay, 2)
    fin[0] = stay[:, 0:HALF] + jnp.where(zh == 0, 0.0, came)
    fin[1] = stay[:, HALF:STAY]
    loads[6].wait()
    swap = remote(fin.at[1 - c], fin_in.at[0], f_s.at[0], f_r.at[0], partner)
    swap.start()
    out[0, :, mine] = fin[c] - tgt[:, mine]
    swap.wait_recv()
    out[0, :, theirs] = fin_in[0] - tgt[:, theirs]
    swap.wait_send()
    for u in range(4):
        h, lo, mid, hi, r0, r1, (n, wide) = unit(u)
        q0, q1 = h * PER + r0 // 4, h * PER + r1 // 4
        take(xs.at[u, :, 0:n, 0:wide], rx_s.at[u])
        take(zs.at[q0:min(q1, OWN) if lo == 0 else q1, :, lo:hi], rz_s.at[u])


def body(*args):
    f32, bf16 = jnp.float32, jnp.bfloat16
    dma = pltpu.SemaphoreType.DMA
    v = pltpu.VMEM
    return pl.pallas_call(
        kernel,
        out_shape=jax.ShapeDtypeStruct((1, 4, D), f32),
        in_specs=[pl.BlockSpec(memory_space=pl.ANY)] * 7,
        out_specs=pl.BlockSpec(memory_space=pltpu.VMEM),
        scratch_shapes=[
            v((4, D), f32),
            v((D, FEATS), bf16),
            v((1, FEATS), f32),
            v((1, FEATS), f32),
            v((4, D), f32),
            v((4, FEATS, HALF), bf16),
            v((NQ, 4, GA), bf16),
            v((8, 8, 4, GB), bf16),
            v((4, GROUP, STAY), bf16),
            v((4, GROUP, STAY), bf16),
            v((NH, HR, D), bf16),
            v((NH, HR, FEATS), bf16),
            v((NH, HR, FEATS), bf16),
            v((NH, HR, W3), f32),
            v((4, 6, XR, HALF), bf16),
            v((4, 6, XR, HALF), bf16),
            v((NQ, 4, W3), bf16),
            v((NQ, 4, W3), bf16),
            v((4, STAY), f32),
            v((2, 4, HALF), f32),
            v((1, 4, HALF), f32),
            dma((6,)), dma((1,)), dma((NG,)), dma((1,)), dma((1,)), dma((1,)), dma((NH,)), dma((1,)), dma((4,)),
            dma((1,)), dma((NH,)), dma((1,)), dma((1,)), dma((1,)), dma((NH,)), dma((4,)), dma((4, 3)),
            dma((4,)), dma((4,)), dma((1,)), dma((1,)),
        ],
        compiler_params=pltpu.CompilerParams(
            collective_id=0, has_side_effects=True, vmem_limit_bytes=56 * 2**20
        ),
    )(*args)


def solution(mesh):
    return jax.shard_map(
        body,
        mesh=mesh,
        in_specs=(
            P("layer", "feat", None),
            P("layer", None, "feat"),
            P("layer", "feat"),
            P("layer", "feat"),
            P("layer", "feat", None),
            P("layer", "feat", None),
            P("layer", "feat", None),
        ),
        out_specs=P("layer", "feat", None),
        check_vma=False,
    )
```
